32 devices in a mesh: body: 4 (over z), mort: 8 (over y, x, core).
Axes of the slice: x: 2, y: 2, z: 4, core: 2. Of those that a mesh axis runs over, the one named last changes fastest.
Arguments:
- displacement: float32 [3, 64, 256, 128], P(None, 'body', 'mort'), may hold values from -6 to 6
- body_load: float32 [3, 64, 256, 128], P(None, 'body', 'mort'), may hold values from -6 to 6
- stiffness: float32 [64, 256, 128], P('body', 'mort'), may hold values from 0.5 to 4
- initial_gap: float32 [4096, 128], P(('body', 'mort')), may hold values from -6 to 6
- weights: float32 [4096, 128], P(('body', 'mort')), may hold values from 0.05 to 1
- basis_values: float32 [4096, 4, 128], P(('body', 'mort')), may hold values from 0 to 1
- point_cell: int32 [4096, 128], P(('body', 'mort')), may hold values from 0 to 511
- point_segment: int32 [4096, 128], P(('body', 'mort')), may hold values from 0 to 255
- block_owner: int32 [4096, 1], P(('body', 'mort')), may hold values from 0 to 7; in each aligned block of 128 rows (0 to 127, 128 to 255, ...) at most 64 rows name the same one
- multipliers: float32 [4, 8192], P(None, ('body', 'mort')), may hold values from 0 to 2
- block_inverse: float32 [4, 4, 8192], P(None, None, ('body', 'mort')), may hold values from -0.9 to 1
Outputs:
- body_residual: float32 [3, 64, 256, 128], P(None, 'body', 'mort')
- new_multipliers: float32 [4, 8192], P(None, ('body', 'mort'))
The draws below stay inside these ranges and needn't reach their ends.
Inputs may be any that keep to these rules, and one draw needn't show every extreme that they name: `block_owner`: among the 128 blocks of one device each owner is named at most 64 times.
All inputs are finite; a program needn't handle non-finite values.
Results may differ from the reference program's by a relative error of at most 0.000098.
Values sent between devices are 32-bit elements; how exact they have to be, the bound alone decides.
A program may use at most 128 MiB of HBM per device.

```python
import math
import jax
import jax.numpy as jnp
import numpy as np

CX = 16
CY = 32
NZ = 128
BLK_DEV = 128
SEG_DEV = 256
PTS = 128
NM = 4
NX = 64
NY = 256
NBLK = 4096
NSEG = 8192
CAP = 64
N_MORT = 8


def draw_block_inverse(key, part):
    first, second = jax.random.split(jax.random.fold_in(key, 17))
    scales = jnp.exp(jax.random.uniform(first, (NSEG,), jnp.float32, math.log(0.2), 0.0))
    offdiag = jnp.clip(0.3 * jax.random.normal(second, (NM, NM, NSEG), jnp.float32), -0.9, 0.9)
    identity = jnp.eye(NM, dtype=jnp.float32)[:, :, None]
    return (identity * scales[None, None, :] + (1.0 - identity) * offdiag * scales[None, None, :]).astype(jnp.float32)


def place_ends(result, key, smallest, high):
    dims = result.shape
    place = [jax.random.randint(jax.random.fold_in(key, axis), (), 0, dims[axis]) for axis in range(len(dims))]
    result = result.at[tuple(place)].set(smallest)
    longest = dims.index(max(dims))
    place[longest] = (place[longest] + 1) % dims[longest]
    return result.at[tuple(place)].set(high)


def shard_levels(rng, shape, pieces, least, largest):
    factor_of = 1.0
    for dim, parts in pieces:
        draws = jax.random.uniform(jax.random.fold_in(jax.random.fold_in(rng, 6), dim), (parts,), jnp.float32, least / len(pieces), largest / len(pieces))
        factor_of = factor_of * jnp.repeat(jnp.exp(draws), shape[dim] // parts).reshape((-1,) + (1,) * (len(shape) - 1 - dim))
    return factor_of


def deal_out(key, own, number, rows, amount, top, reach, slope):
    sequence = jax.random.permutation(key, amount)
    heavy_load, common = portions_of(amount, rows * top, reach, slope, True), portions_of(amount, rows * top, reach, slope, False)
    places = jnp.arange(amount)

    def named(tallies, turn):
        used = int((tallies > 0).sum())
        fixed = max(1, used // 4)
        moved = fixed + (places - fixed + turn * (used - fixed)) % max(1, amount - fixed)
        return jnp.zeros((amount,), jnp.int32).at[sequence[jnp.where(places < fixed, places, moved)]].set(jnp.asarray(tallies, jnp.int32))

    tallies = jnp.where(number % 4 == 0, named(heavy_load, number // 4), named(common, number - number // 4 - 1))
    mixed = jax.random.permutation(jax.random.fold_in(own, 3), amount)
    source_of, taker = mixed[0:amount // 2 * 2:2], mixed[1:amount // 2 * 2:2]
    room = jnp.minimum(tallies[source_of] - 1, reach - tallies[taker]) // 2
    room = jnp.where((source_of == sequence[0]) | (taker == sequence[0]) | (tallies[taker] == 0), 0, jnp.maximum(room, 0))
    moved = jax.random.randint(jax.random.fold_in(own, 4), (amount // 2,), 0, 1 << 20) % (room + 1)
    tallies = tallies.at[source_of].add(-moved).at[taker].add(moved)
    members = jnp.searchsorted(jnp.cumsum(tallies), jnp.arange(rows * top), side="right").astype(jnp.int32)
    table = members.reshape(top, rows).T
    table = table[jax.random.permutation(jax.random.fold_in(own, 1), rows)]
    turn = jax.random.randint(jax.random.fold_in(own, 2), (rows, 1), 0, top)
    return jnp.take_along_axis(table, (jnp.arange(top)[None, :] + turn) % top, axis=1)


def portions_of(count, total, limit, lean, full):
    weights = [(1 << 20) // math.isqrt(rank ** lean) + 1 for rank in range(1, count + 1)]
    largest = limit if full else min(limit, max(-(-total // count), total * weights[0] // sum(weights)))
    least = 1 if total - largest >= count - 1 else 0
    holding, spare = [largest] + [least] * (count - 1), total - largest - least * (count - 1)
    while spare > 0:
        free = [i for i in range(1, count) if holding[i] < largest] or [i for i in range(1, count) if holding[i] < limit]
        pool, budget = sum([weights[i] for i in free]), spare
        for i in free:
            extra = min(limit - holding[i], max(1, budget * weights[i] // pool), spare)
            holding[i] = holding[i] + extra
            spare = spare - extra
    return np.array(holding)


def scatter_about(own_key, shape, deviation, limit, shards=(), kind=jnp.bfloat16):
    entries = deviation * jax.random.normal(own_key, shape, jnp.float32)
    if shards:
        entries = entries * shard_levels(own_key, shape, shards, -0.22, 0.18)
    return jnp.clip(entries, -limit, limit).astype(kind)


def setup_inputs(seed: int = 0) -> dict:
    arg_keys = jax.random.split(jax.random.key(seed), 12)
    displacement = scatter_about(arg_keys[0], (3, NX, NY, NZ), 1.0, 6.0, ((1, 4), (2, 8)), jnp.float32)
    body_load = scatter_about(arg_keys[1], (3, NX, NY, NZ), 1.0, 6.0, ((1, 4), (2, 8)), jnp.float32)
    stiffness = jnp.clip(jnp.exp(math.log(4.0) - 2.0794415 * jax.random.uniform(arg_keys[2], (NX, NY, NZ), jnp.float32) ** shard_levels(arg_keys[2], (NX, NY, NZ), ((0, 4), (1, 8)), -0.2, 0.2)), 0.5, 4.0)
    initial_gap = scatter_about(arg_keys[3], (NBLK, PTS), 1.0, 6.0, ((0, 32),), jnp.float32)
    weights = jnp.clip(jnp.exp(math.log(1.0) - 2.9957323 * jax.random.uniform(arg_keys[4], (NBLK, PTS), jnp.float32) ** shard_levels(arg_keys[4], (NBLK, PTS), ((0, 32),), -0.2, 0.2)), 0.05, 1.0)
    basis_values = jnp.clip(1.0 * jax.random.uniform(arg_keys[5], (NBLK, NM, PTS), jnp.float32) ** shard_levels(arg_keys[5], (NBLK, NM, PTS), ((0, 32),), -0.2, 0.2), 0.0, 1.0)
    point_cell = place_ends(jax.random.randint(arg_keys[6], (NBLK, PTS), 0, CX * CY), jax.random.fold_in(arg_keys[6], 1), 0, (CX * CY) - 1).astype(jnp.int32)
    point_segment = place_ends(jax.random.randint(arg_keys[7], (NBLK, PTS), 0, SEG_DEV), jax.random.fold_in(arg_keys[7], 1), 0, SEG_DEV - 1).astype(jnp.int32)
    block_owner_keys = jax.random.split(jax.random.fold_in(arg_keys[8], 1), NBLK // BLK_DEV)
    block_owner_turns = jax.random.permutation(jax.random.fold_in(arg_keys[8], 3), NBLK // BLK_DEV)
    block_owner = jax.vmap(lambda own, number: deal_out(jax.random.fold_in(arg_keys[8], 2), own, number, BLK_DEV, N_MORT, 1, CAP, 2))(block_owner_keys, block_owner_turns).reshape((NBLK, 1))
    multipliers = jnp.clip(2.0 * jax.random.uniform(arg_keys[9], (NM, NSEG), jnp.float32) ** shard_levels(arg_keys[9], (NM, NSEG), ((1, 32),), -0.2, 0.2), 0.0, 2.0)
    block_inverse = draw_block_inverse(jax.random.fold_in(arg_keys[11], 71), 0)
    return {"displacement": displacement, "body_load": body_load, "stiffness": stiffness, "initial_gap": initial_gap, "weights": weights, "basis_values": basis_values, "point_cell": point_cell, "point_segment": point_segment, "block_owner": block_owner, "multipliers": multipliers, "block_inverse": block_inverse}


def reference(displacement, body_load, stiffness, initial_gap, weights, basis_values, point_cell, point_segment, block_owner, multipliers, block_inverse):
    mort_count = NY // CY
    blocks = jnp.arange(initial_gap.shape[0], dtype=jnp.int32)
    anchors = blocks // BLK_DEV
    body_row = (anchors // mort_count)[:, None]
    mort_col = (anchors % mort_count)[:, None]
    cell_x = (body_row * CX + point_cell // CY).astype(jnp.int32)
    cell_y = (mort_col * CY + point_cell % CY).astype(jnp.int32)
    point_gap = initial_gap + displacement[2, :, :, 0][cell_x, cell_y]
    integrand = weights[:, None, :] * basis_values * point_gap[:, None, :]
    global_segment = ((body_row * mort_count + block_owner[:, 0:1]) * SEG_DEV + point_segment).astype(jnp.int32)
    flat_terms = jnp.transpose(integrand, (0, 2, 1)).reshape(-1, NM)
    integrals = jax.ops.segment_sum(flat_terms, global_segment.reshape(-1), num_segments=NSEG).T
    applied = jnp.sum(block_inverse * integrals[None, :, :], axis=1)
    updated = jnp.maximum(multipliers - applied, 0.0)
    change = updated - multipliers
    picked = change.T[global_segment]
    pressure = jnp.sum(picked * jnp.transpose(basis_values, (0, 2, 1)), axis=2)
    traction = jnp.zeros((NX, NY), jnp.float32).at[cell_x, cell_y].add(weights * pressure)
    padded = jnp.pad(displacement, ((0, 0), (1, 1), (1, 1), (1, 1)))
    beside = padded[:, 2:, 1:-1, 1:-1] + padded[:, :-2, 1:-1, 1:-1]
    beside = beside + padded[:, 1:-1, 2:, 1:-1] + padded[:, 1:-1, :-2, 1:-1]
    beside = beside + padded[:, 1:-1, 1:-1, 2:] + padded[:, 1:-1, 1:-1, :-2]
    stiff_force = (6.0 + stiffness)[None] * displacement - beside
    residual = body_load - stiff_force
    residual = residual.at[2, :, :, 0].add(traction)
    return residual, updated
```

```python
import functools

import jax
import jax.numpy as jnp
from jax import lax
from jax.experimental import pallas as pl
from jax.experimental.pallas import tpu as pltpu
from jax.sharding import PartitionSpec as P

LANES = 128
ROWS = 8
PIECES = 3
VMEM = pl.BlockSpec(memory_space=pltpu.VMEM)
SMEM = pl.BlockSpec(memory_space=pltpu.SMEM)
ANY = pl.BlockSpec(memory_space=pl.ANY)


def pieces_of(value):
    out = []
    for _ in range(PIECES - 1):
        part = value.astype(jnp.bfloat16).astype(jnp.float32)
        out.append(part)
        value = value - part
    return out + [value]


def lane_gather(table, index):
    return jnp.take_along_axis(table, index, axis=1, mode="promise_in_bounds")


def gather_rows(rows, index):
    row, lane = index // LANES, index % LANES
    value = None
    for number, piece in enumerate(rows):
        got = lane_gather(jnp.broadcast_to(piece, index.shape), lane)
        value = got if value is None else jnp.where(row == number, got, value)
    return value


def nt_dot(a, b):
    return lax.dot_general(a, b, (((1,), (1,)), ((), ())), preferred_element_type=jnp.float32)


def shares_kernel(
    count, modes, disp_ref, gap_ref, weight_ref, basis_ref, cell_ref, seg_ref, owner_ref,
    partial_ref, face_ref, terms, acc,
):
    _, cells_x, cells_y, _ = disp_ref.shape
    blocks = gap_ref.shape[0]
    segments = partial_ref.shape[2]
    pad = terms.shape[0] // blocks
    face_ref[0] = disp_ref[:, :, cells_y - 1, :]
    face_ref[1] = disp_ref[:, :, 0, :]
    per = LANES // cells_y
    lane = lax.broadcasted_iota(jnp.int32, (cells_y, LANES), 1)
    columns = []
    for j in range(per):
        column = jnp.zeros((cells_y, LANES), jnp.float32)
        for r in range(cells_x // per):
            values = disp_ref[2, r * per + j, :, :][:, 0:1]
            column = jnp.where(lane == r, values, column)
        columns.append(column)
    table = jnp.concatenate(columns, axis=0).T
    surface = [table[r : r + 1, :] for r in range(cells_x // per)]

    zero = jnp.zeros((ROWS, LANES), jnp.float32)

    def prepare(t, _):
        first = pl.multiple_of(t * ROWS, ROWS)
        rows = pl.ds(first, ROWS)
        gap = gap_ref[rows, :] + gather_rows(surface, cell_ref[rows, :])
        weights = weight_ref[rows, :]
        for k in range(modes):
            basis = basis_ref[pl.ds(first * modes + k, ROWS, stride=modes), :]
            for s, piece in enumerate(pieces_of(weights * basis * gap)):
                terms[pl.ds(first * pad + s * modes + k, ROWS, stride=pad), :] = piece
        for k in range(PIECES * modes, pad):
            terms[pl.ds(first * pad + k, ROWS, stride=pad), :] = zero
        return 0

    lax.fori_loop(0, blocks // ROWS, prepare, 0, unroll=2)
    acc[...] = jnp.zeros_like(acc)
    ids = lax.broadcasted_iota(jnp.int32, (segments, LANES), 0)

    def add(t, _):
        first = pl.multiple_of(t * ROWS, ROWS)
        left, right = [], []
        for i in range(ROWS):
            item = terms[pl.ds(pl.multiple_of((first + i) * pad, pad), pad), :].astype(jnp.bfloat16)
            owner = owner_ref[first + i]
            left.append(
                jnp.concatenate(
                    [jnp.where(owner == o, item, jnp.zeros_like(item)) for o in range(count)], axis=0
                )
            )
            segs = seg_ref[pl.ds(first + i, 1), :]
            right.append(jnp.where(segs == ids, 1.0, 0.0).astype(jnp.bfloat16))
        acc[...] += nt_dot(jnp.concatenate(left, axis=1), jnp.concatenate(right, axis=1))
        return 0

    lax.fori_loop(0, blocks // ROWS, add, 0)
    for o in range(count):
        total = acc[pl.ds(o * pad, pad), :]
        value = total[0:modes]
        for s in range(1, PIECES):
            value = value + total[s * modes : (s + 1) * modes]
        partial_ref[o] = value


def exchange_kernel(
    partial_ref, mult_ref, inv_ref, face_ref, disp_ref,
    changes_ref, updated_ref, xhalo_ref, yhalo_ref,
    landed, send1, recv1, send2, recv2, sendx, recvx, sendy, recvy,
):
    count, nb = lax.axis_size("mort"), lax.axis_size("body")
    me, mb = lax.axis_index("mort"), lax.axis_index("body")
    cells_x = disp_ref.shape[1]
    barrier = pltpu.get_barrier_semaphore()
    for j in range(1, count):
        pl.semaphore_signal(
            barrier, inc=1, device_id={"mort": lax.rem(me + j, count)},
            device_id_type=pl.DeviceIdType.MESH,
        )
    for j in (1, nb - 1):
        pl.semaphore_signal(
            barrier, inc=1, device_id={"body": lax.rem(mb + j, nb)},
            device_id_type=pl.DeviceIdType.MESH,
        )
    pl.semaphore_wait(barrier, count + 1)

    def share(j):
        target = lax.rem(me + j, count)
        return pltpu.make_async_remote_copy(
            src_ref=partial_ref.at[target], dst_ref=landed.at[j],
            send_sem=send1.at[j], recv_sem=recv1.at[j],
            device_id={"mort": target}, device_id_type=pl.DeviceIdType.MESH,
        )

    def xcopy(side):
        return pltpu.make_async_remote_copy(
            src_ref=disp_ref.at[:, cells_x - 1 if side == 0 else 0],
            dst_ref=xhalo_ref.at[side],
            send_sem=sendx.at[side], recv_sem=recvx.at[side],
            device_id={"body": lax.rem(mb + (1 if side == 0 else nb - 1), nb)},
            device_id_type=pl.DeviceIdType.MESH,
        )

    def ycopy(side):
        return pltpu.make_async_remote_copy(
            src_ref=face_ref.at[side], dst_ref=yhalo_ref.at[side],
            send_sem=sendy.at[side], recv_sem=recvy.at[side],
            device_id={"mort": lax.rem(me + (1 if side == 0 else count - 1), count)},
            device_id_type=pl.DeviceIdType.MESH,
        )

    shares = [share(j) for j in range(1, count)]
    for copy in shares:
        copy.start()
    halos = []
    for make, place, size, ref in ((xcopy, mb, nb, xhalo_ref), (ycopy, me, count, yhalo_ref)):
        for side in range(2):
            sends = place < size - 1 if side == 0 else place > 0
            takes = place > 0 if side == 0 else place < size - 1
            halos.append((make, side, sends, takes))

            @pl.when(sends)
            def _():
                make(side).start()

            @pl.when(jnp.logical_not(takes))
            def _():
                ref[side] = jnp.zeros(ref.shape[1:], ref.dtype)

    total = partial_ref[me]
    for j in range(1, count):
        shares[j - 1].wait_recv()
        total = total + landed[j]
    applied = inv_ref[:, 0, :] * total[0:1, :]
    for l in range(1, total.shape[0]):
        applied = applied + inv_ref[:, l, :] * total[l : l + 1, :]
    old = mult_ref[...]
    updated = jnp.maximum(old - applied, 0.0)
    updated_ref[...] = updated
    changes_ref[me] = updated - old

    def spread(j):
        return pltpu.make_async_remote_copy(
            src_ref=changes_ref.at[me], dst_ref=changes_ref.at[me],
            send_sem=send2.at[j], recv_sem=recv2.at[j],
            device_id={"mort": lax.rem(me + j, count)}, device_id_type=pl.DeviceIdType.MESH,
        )

    def arrival(j):
        source = lax.rem(me + count - j, count)
        return pltpu.make_async_remote_copy(
            src_ref=changes_ref.at[me], dst_ref=changes_ref.at[source],
            send_sem=send2.at[j], recv_sem=recv2.at[j],
            device_id={"mort": lax.rem(me + j, count)}, device_id_type=pl.DeviceIdType.MESH,
        )

    for j in range(1, count):
        spread(j).start()
    for copy in shares:
        copy.wait_send()
    for make, side, sends, takes in halos:

        @pl.when(sends)
        def _():
            make(side).wait_send()

        @pl.when(takes)
        def _():
            make(side).wait_recv()

    for j in range(1, count):
        spread(j).wait_send()
        arrival(j).wait_recv()


def residual_kernel(
    disp_ref, load_ref, stiff_ref, weight_ref, basis_ref, cell_ref, seg_ref, owner_ref,
    changes_ref, new_ref, xhalo_ref, yhalo_ref,
    out_ref, updated_ref, loads,
):
    parts, cells_x, cells_y, nz = disp_ref.shape
    blocks = weight_ref.shape[0]
    count, modes, segments = changes_ref.shape
    updated_ref[...] = new_ref[...]

    def pressures(t, _):
        first = pl.multiple_of(t * ROWS, ROWS)
        rows = pl.ds(first, ROWS)
        owner = jnp.broadcast_to(owner_ref[rows, :], (ROWS, LANES))
        segs = seg_ref[rows, :]
        masks = [owner == o for o in range(count)]
        pressure = None
        for k in range(modes):
            pieces = []
            for h in range(segments // LANES):
                piece = jnp.zeros((ROWS, LANES), jnp.float32)
                for o in range(count):
                    row = changes_ref[o, k : k + 1, h * LANES : (h + 1) * LANES]
                    piece = jnp.where(masks[o], row, piece)
                pieces.append(piece)
            basis = basis_ref[pl.ds(first * modes + k, ROWS, stride=modes), :]
            term = basis * gather_rows(pieces, segs)
            pressure = term if pressure is None else pressure + term
        loads[rows, :] = weight_ref[rows, :] * pressure
        return 0

    lax.fori_loop(0, blocks // ROWS, pressures, 0)
    xs = lax.broadcasted_iota(jnp.int32, (cells_x, LANES), 0)
    ys = lax.broadcasted_iota(jnp.int32, (cells_y, LANES), 0)

    def spread(t, acc):
        first = t * ROWS
        left, right = [], []
        for i in range(ROWS):
            cell = cell_ref[pl.ds(first + i, 1), :]
            at_x, at_y = cell // cells_y, cell % cells_y
            left.append(jnp.where(at_y == ys, 1.0, 0.0).astype(jnp.bfloat16))
            value = jnp.where(at_x == xs, loads[pl.ds(first + i, 1), :], 0.0)
            right.append(jnp.concatenate([p.astype(jnp.bfloat16) for p in pieces_of(value)], axis=0))
        return acc + nt_dot(jnp.concatenate(left, axis=1), jnp.concatenate(right, axis=1))

    acc = lax.fori_loop(
        0, blocks // ROWS, spread, jnp.zeros((cells_y, PIECES * cells_x), jnp.float32)
    )
    lane = lax.broadcasted_iota(jnp.int32, (cells_y, nz), 1)
    row = lax.broadcasted_iota(jnp.int32, (cells_y, nz), 0)
    for x in range(cells_x):
        diagonal = 6.0 + stiff_ref[x]
        for i in range(parts):
            here = disp_ref[i, x]
            low = disp_ref[i, x - 1] if x > 0 else xhalo_ref[0, i]
            high = disp_ref[i, x + 1] if x < cells_x - 1 else xhalo_ref[1, i]
            below = jnp.where(row == 0, yhalo_ref[0, i, x : x + 1, :], pltpu.roll(here, 1, 0))
            above = jnp.where(
                row == cells_y - 1, yhalo_ref[1, i, x : x + 1, :], pltpu.roll(here, cells_y - 1, 0)
            )
            left = jnp.where(lane == 0, 0.0, pltpu.roll(here, 1, 1))
            right = jnp.where(lane == nz - 1, 0.0, pltpu.roll(here, nz - 1, 1))
            beside = high + low + above + below + right + left
            residual = load_ref[i, x] - (diagonal * here - beside)
            if i == 2:
                traction = acc[:, x : x + 1]
                for s in range(1, PIECES):
                    traction = traction + acc[:, s * cells_x + x : s * cells_x + x + 1]
                residual = jnp.where(lane == 0, residual + traction, residual)
            out_ref[i, x] = residual


def body(
    displacement, body_load, stiffness, initial_gap, weights, basis_values, point_cell,
    point_segment, block_owner, multipliers, block_inverse,
):
    parts, cells_x, cells_y, nz = displacement.shape
    blocks, points = initial_gap.shape
    modes, segments = multipliers.shape
    count = lax.axis_size("mort")
    f32 = jnp.float32
    basis = basis_values.reshape(blocks * modes, points)
    pad = -(-PIECES * modes // 16) * 16
    shape = jax.ShapeDtypeStruct
    partial, faces = pl.pallas_call(
        functools.partial(shares_kernel, count, modes),
        name="shares",
        out_shape=(
            shape((count, modes, segments), f32),
            shape((2, parts, cells_x, nz), f32),
        ),
        in_specs=[VMEM] * 6 + [SMEM],
        out_specs=(VMEM, VMEM),
        scratch_shapes=[
            pltpu.VMEM((blocks * pad, LANES), f32),
            pltpu.VMEM((count * pad, segments), f32),
        ],
    )(
        displacement, initial_gap, weights, basis, point_cell, point_segment,
        block_owner.reshape(blocks),
    )
    dma = pltpu.SemaphoreType.DMA
    changes, new, xhalo, yhalo = pl.pallas_call(
        exchange_kernel,
        name="exchange",
        out_shape=(
            shape((count, modes, segments), f32),
            shape((modes, segments), f32),
            shape((2, parts, cells_y, nz), f32),
            shape((2, parts, cells_x, nz), f32),
        ),
        in_specs=[VMEM] * 4 + [ANY],
        out_specs=(VMEM,) * 4,
        scratch_shapes=[pltpu.VMEM((count, modes, segments), f32)]
        + [dma((count,))] * 4
        + [dma((2,))] * 4,
        compiler_params=pltpu.CompilerParams(collective_id=0, has_side_effects=True),
    )(partial, multipliers, block_inverse, faces, displacement)
    return pl.pallas_call(
        residual_kernel,
        name="residual",
        out_shape=(
            shape(displacement.shape, f32),
            shape((modes, segments), f32),
        ),
        in_specs=[VMEM] * 12,
        out_specs=(VMEM, VMEM),
        scratch_shapes=[pltpu.VMEM((blocks, LANES), f32)],
    )(
        displacement, body_load, stiffness, weights, basis, point_cell, point_segment,
        block_owner, changes, new, xhalo, yhalo,
    )


def solution(mesh):
    return jax.shard_map(
        body,
        mesh=mesh,
        in_specs=(
            P(None, "body", "mort", None),
            P(None, "body", "mort", None),
            P("body", "mort", None),
            P(("body", "mort"), None),
            P(("body", "mort"), None),
            P(("body", "mort"), None, None),
            P(("body", "mort"), None),
            P(("body", "mort"), None),
            P(("body", "mort"), None),
            P(None, ("body", "mort")),
            P(None, None, ("body", "mort")),
        ),
        out_specs=(P(None, "body", "mort", None), P(None, ("body", "mort"))),
        check_vma=False,
    )
```

```python
import jax
import jax.numpy as jnp
from jax import lax
from jax.experimental import pallas as pl
from jax.experimental.pallas import tpu as pltpu
from jax.sharding import PartitionSpec as P

LANES = 128
ROWS = 8
PIECES = 3
VMEM = pl.BlockSpec(memory_space=pltpu.VMEM)
SMEM = pl.BlockSpec(memory_space=pltpu.SMEM)


def pieces_of(value):
    out = []
    for _ in range(PIECES - 1):
        part = value.astype(jnp.bfloat16).astype(jnp.float32)
        out.append(part)
        value = value - part
    return out + [value]


def lane_gather(table, index):
    return jnp.take_along_axis(table, index, axis=1, mode="promise_in_bounds")


def gather_rows(rows, index):
    row, lane = index // LANES, index % LANES
    value = None
    for number, piece in enumerate(rows):
        got = lane_gather(jnp.broadcast_to(piece, index.shape), lane)
        value = got if value is None else jnp.where(row == number, got, value)
    return value


def nt_dot(a, b):
    return lax.dot_general(a, b, (((1,), (1,)), ((), ())), preferred_element_type=jnp.float32)


def make_shares(
    disp_ref, gap_ref, weight_ref, basis_ref, cell_ref, seg_ref, owner_ref,
    partial_ref, terms, acc,
):
    count, modes, _ = partial_ref.shape
    _, cells_x, cells_y, _ = disp_ref.shape
    blocks = gap_ref.shape[0]
    segments = partial_ref.shape[2]
    pad = terms.shape[0] // blocks
    per = LANES // cells_y
    lane = lax.broadcasted_iota(jnp.int32, (cells_y, LANES), 1)
    columns = []
    for j in range(per):
        column = jnp.zeros((cells_y, LANES), jnp.float32)
        for r in range(cells_x // per):
            values = disp_ref[2, r * per + j, :, :][:, 0:1]
            column = jnp.where(lane == r, values, column)
        columns.append(column)
    table = jnp.concatenate(columns, axis=0).T
    surface = [table[r : r + 1, :] for r in range(cells_x // per)]

    zero = jnp.zeros((ROWS, LANES), jnp.float32)

    def prepare(t, _):
        first = pl.multiple_of(t * ROWS, ROWS)
        rows = pl.ds(first, ROWS)
        gap = gap_ref[rows, :] + gather_rows(surface, cell_ref[rows, :])
        weights = weight_ref[rows, :]
        for k in range(modes):
            basis = basis_ref[pl.ds(first * modes + k, ROWS, stride=modes), :]
            for s, piece in enumerate(pieces_of(weights * basis * gap)):
                terms[pl.ds(first * pad + s * modes + k, ROWS, stride=pad), :] = piece
        for k in range(PIECES * modes, pad):
            terms[pl.ds(first * pad + k, ROWS, stride=pad), :] = zero
        return 0

    lax.fori_loop(0, blocks // ROWS, prepare, 0, unroll=2)
    acc[...] = jnp.zeros_like(acc)
    ids = lax.broadcasted_iota(jnp.int32, (segments, LANES), 0)

    def add(t, _):
        first = pl.multiple_of(t * ROWS, ROWS)
        left, right = [], []
        for i in range(ROWS):
            item = terms[pl.ds(pl.multiple_of((first + i) * pad, pad), pad), :].astype(jnp.bfloat16)
            owner = owner_ref[first + i]
            left.append(
                jnp.concatenate(
                    [jnp.where(owner == o, item, jnp.zeros_like(item)) for o in range(count)], axis=0
                )
            )
            segs = seg_ref[pl.ds(first + i, 1), :]
            right.append(jnp.where(segs == ids, 1.0, 0.0).astype(jnp.bfloat16))
        acc[...] += nt_dot(jnp.concatenate(left, axis=1), jnp.concatenate(right, axis=1))
        return 0

    lax.fori_loop(0, blocks // ROWS, add, 0)
    for o in range(count):
        total = acc[pl.ds(o * pad, pad), :]
        value = total[0:modes]
        for s in range(1, PIECES):
            value = value + total[s * modes : (s + 1) * modes]
        partial_ref[o] = value


def exchange_kernel(
    disp_ref, gap_ref, weight_ref, basis_ref, cell_ref, seg_ref, owner_ref, mult_ref, inv_ref,
    changes_ref, updated_ref, xhalo_ref, yhalo_ref,
    terms, acc, partial_ref, face_ref, landed, send1, recv1, send2, recv2, sendx, recvx, sendy, recvy,
):
    count, nb = lax.axis_size("mort"), lax.axis_size("body")
    me, mb = lax.axis_index("mort"), lax.axis_index("body")
    cells_x = disp_ref.shape[1]
    barrier = pltpu.get_barrier_semaphore()
    for j in range(1, count):
        pl.semaphore_signal(
            barrier, inc=1, device_id={"mort": lax.rem(me + j, count)},
            device_id_type=pl.DeviceIdType.MESH,
        )
    for j in (1, nb - 1):
        pl.semaphore_signal(
            barrier, inc=1, device_id={"body": lax.rem(mb + j, nb)},
            device_id_type=pl.DeviceIdType.MESH,
        )
    cells_y = disp_ref.shape[2]
    face_ref[0] = disp_ref[:, :, cells_y - 1, :]
    face_ref[1] = disp_ref[:, :, 0, :]
    make_shares(
        disp_ref, gap_ref, weight_ref, basis_ref, cell_ref, seg_ref, owner_ref,
        partial_ref, terms, acc,
    )
    pl.semaphore_wait(barrier, count + 1)

    def share(j):
        target = lax.rem(me + j, count)
        return pltpu.make_async_remote_copy(
            src_ref=partial_ref.at[target], dst_ref=landed.at[j],
            send_sem=send1.at[j], recv_sem=recv1.at[j],
            device_id={"mort": target}, device_id_type=pl.DeviceIdType.MESH,
        )

    def xcopy(side):
        return pltpu.make_async_remote_copy(
            src_ref=disp_ref.at[:, cells_x - 1 if side == 0 else 0],
            dst_ref=xhalo_ref.at[side],
            send_sem=sendx.at[side], recv_sem=recvx.at[side],
            device_id={"body": lax.rem(mb + (1 if side == 0 else nb - 1), nb)},
            device_id_type=pl.DeviceIdType.MESH,
        )

    def ycopy(side):
        return pltpu.make_async_remote_copy(
            src_ref=face_ref.at[side], dst_ref=yhalo_ref.at[side],
            send_sem=sendy.at[side], recv_sem=recvy.at[side],
            device_id={"mort": lax.rem(me + (1 if side == 0 else count - 1), count)},
            device_id_type=pl.DeviceIdType.MESH,
        )

    shares = [share(j) for j in range(1, count)]
    for copy in shares:
        copy.start()
    halos = []
    for make, place, size, ref in ((xcopy, mb, nb, xhalo_ref), (ycopy, me, count, yhalo_ref)):
        for side in range(2):
            sends = place < size - 1 if side == 0 else place > 0
            takes = place > 0 if side == 0 else place < size - 1
            halos.append((make, side, sends, takes))

            @pl.when(sends)
            def _():
                make(side).start()

            @pl.when(jnp.logical_not(takes))
            def _():
                ref[side] = jnp.zeros(ref.shape[1:], ref.dtype)

    total = partial_ref[me]
    for j in range(1, count):
        shares[j - 1].wait_recv()
        total = total + landed[j]
    applied = inv_ref[:, 0, :] * total[0:1, :]
    for l in range(1, total.shape[0]):
        applied = applied + inv_ref[:, l, :] * total[l : l + 1, :]
    old = mult_ref[...]
    updated = jnp.maximum(old - applied, 0.0)
    updated_ref[...] = updated
    changes_ref[me] = updated - old

    def spread(j):
        return pltpu.make_async_remote_copy(
            src_ref=changes_ref.at[me], dst_ref=changes_ref.at[me],
            send_sem=send2.at[j], recv_sem=recv2.at[j],
            device_id={"mort": lax.rem(me + j, count)}, device_id_type=pl.DeviceIdType.MESH,
        )

    def arrival(j):
        source = lax.rem(me + count - j, count)
        return pltpu.make_async_remote_copy(
            src_ref=changes_ref.at[me], dst_ref=changes_ref.at[source],
            send_sem=send2.at[j], recv_sem=recv2.at[j],
            device_id={"mort": lax.rem(me + j, count)}, device_id_type=pl.DeviceIdType.MESH,
        )

    for j in range(1, count):
        spread(j).start()
    for copy in shares:
        copy.wait_send()
    for make, side, sends, takes in halos:

        @pl.when(sends)
        def _():
            make(side).wait_send()

        @pl.when(takes)
        def _():
            make(side).wait_recv()

    for j in range(1, count):
        spread(j).wait_send()
        arrival(j).wait_recv()


def residual_kernel(
    disp_ref, load_ref, stiff_ref, weight_ref, basis_ref, cell_ref, seg_ref, owner_ref,
    changes_ref, new_ref, xhalo_ref, yhalo_ref,
    out_ref, updated_ref, loads, owners,
):
    parts, cells_x, cells_y, nz = disp_ref.shape
    blocks = weight_ref.shape[0]
    count, modes, segments = changes_ref.shape
    updated_ref[...] = new_ref[...]
    owners[...] = jnp.broadcast_to(owner_ref[...], (LANES, blocks)).T

    def pressures(t, _):
        first = pl.multiple_of(t * ROWS, ROWS)
        rows = pl.ds(first, ROWS)
        owner = owners[rows, :]
        segs = seg_ref[rows, :]
        masks = [owner == o for o in range(count)]
        pressure = None
        for k in range(modes):
            pieces = []
            for h in range(segments // LANES):
                piece = jnp.zeros((ROWS, LANES), jnp.float32)
                for o in range(count):
                    row = changes_ref[o, k : k + 1, h * LANES : (h + 1) * LANES]
                    piece = jnp.where(masks[o], row, piece)
                pieces.append(piece)
            basis = basis_ref[pl.ds(first * modes + k, ROWS, stride=modes), :]
            term = basis * gather_rows(pieces, segs)
            pressure = term if pressure is None else pressure + term
        loads[rows, :] = weight_ref[rows, :] * pressure
        return 0

    lax.fori_loop(0, blocks // ROWS, pressures, 0)
    xs = lax.broadcasted_iota(jnp.int32, (cells_x, LANES), 0)
    ys = lax.broadcasted_iota(jnp.int32, (cells_y, LANES), 0)

    def spread(t, acc):
        first = t * ROWS
        left, right = [], []
        for i in range(ROWS):
            cell = cell_ref[pl.ds(first + i, 1), :]
            at_x, at_y = cell // cells_y, cell % cells_y
            left.append(jnp.where(at_y == ys, 1.0, 0.0).astype(jnp.bfloat16))
            value = jnp.where(at_x == xs, loads[pl.ds(first + i, 1), :], 0.0)
            right.append(jnp.concatenate([p.astype(jnp.bfloat16) for p in pieces_of(value)], axis=0))
        return acc + nt_dot(jnp.concatenate(left, axis=1), jnp.concatenate(right, axis=1))

    acc = lax.fori_loop(
        0, blocks // ROWS, spread, jnp.zeros((cells_y, PIECES * cells_x), jnp.float32)
    )
    lane = lax.broadcasted_iota(jnp.int32, (cells_y, nz), 1)
    row = lax.broadcasted_iota(jnp.int32, (cells_y, nz), 0)
    for x in range(cells_x):
        diagonal = 6.0 + stiff_ref[x]
        for i in range(parts):
            here = disp_ref[i, x]
            low = disp_ref[i, x - 1] if x > 0 else xhalo_ref[0, i]
            high = disp_ref[i, x + 1] if x < cells_x - 1 else xhalo_ref[1, i]
            below = jnp.where(row == 0, yhalo_ref[0, i, x : x + 1, :], pltpu.roll(here, 1, 0))
            above = jnp.where(
                row == cells_y - 1, yhalo_ref[1, i, x : x + 1, :], pltpu.roll(here, cells_y - 1, 0)
            )
            left = jnp.where(lane == 0, 0.0, pltpu.roll(here, 1, 1))
            right = jnp.where(lane == nz - 1, 0.0, pltpu.roll(here, nz - 1, 1))
            beside = high + low + above + below + right + left
            residual = load_ref[i, x] - (diagonal * here - beside)
            if i == 2:
                traction = acc[:, x : x + 1]
                for s in range(1, PIECES):
                    traction = traction + acc[:, s * cells_x + x : s * cells_x + x + 1]
                residual = jnp.where(lane == 0, residual + traction, residual)
            out_ref[i, x] = residual


def body(
    displacement, body_load, stiffness, initial_gap, weights, basis_values, point_cell,
    point_segment, block_owner, multipliers, block_inverse,
):
    parts, cells_x, cells_y, nz = displacement.shape
    blocks, points = initial_gap.shape
    modes, segments = multipliers.shape
    count = lax.axis_size("mort")
    f32 = jnp.float32
    basis = basis_values.reshape(blocks * modes, points)
    pad = -(-PIECES * modes // 16) * 16
    shape = jax.ShapeDtypeStruct
    dma = pltpu.SemaphoreType.DMA
    changes, new, xhalo, yhalo = pl.pallas_call(
        exchange_kernel,
        name="exchange",
        out_shape=(
            shape((count, modes, segments), f32),
            shape((modes, segments), f32),
            shape((2, parts, cells_y, nz), f32),
            shape((2, parts, cells_x, nz), f32),
        ),
        in_specs=[VMEM] * 6 + [SMEM] + [VMEM] * 2,
        out_specs=(VMEM,) * 4,
        scratch_shapes=[
            pltpu.VMEM((blocks * pad, LANES), f32),
            pltpu.VMEM((count * pad, segments), f32),
            pltpu.VMEM((count, modes, segments), f32),
            pltpu.VMEM((2, parts, cells_x, nz), f32),
            pltpu.VMEM((count, modes, segments), f32),
        ]
        + [dma((count,))] * 4
        + [dma((2,))] * 4,
        compiler_params=pltpu.CompilerParams(
            vmem_limit_bytes=8 << 20, collective_id=0, has_side_effects=True
        ),
    )(
        displacement, initial_gap, weights, basis, point_cell, point_segment,
        block_owner.reshape(blocks), multipliers, block_inverse,
    )
    return pl.pallas_call(
        residual_kernel,
        name="residual",
        compiler_params=pltpu.CompilerParams(vmem_limit_bytes=8 << 20),
        out_shape=(
            shape(displacement.shape, f32),
            shape((modes, segments), f32),
        ),
        in_specs=[VMEM] * 12,
        out_specs=(VMEM, VMEM),
        scratch_shapes=[pltpu.VMEM((blocks, LANES), f32), pltpu.VMEM((blocks, LANES), jnp.int32)],
    )(
        displacement, body_load, stiffness, weights, basis, point_cell, point_segment,
        block_owner.reshape(1, blocks), changes, new, xhalo, yhalo,
    )


def solution(mesh):
    return jax.shard_map(
        body,
        mesh=mesh,
        in_specs=(
            P(None, "body", "mort", None),
            P(None, "body", "mort", None),
            P("body", "mort", None),
            P(("body", "mort"), None),
            P(("body", "mort"), None),
            P(("body", "mort"), None, None),
            P(("body", "mort"), None),
            P(("body", "mort"), None),
            P(("body", "mort"), None),
            P(None, ("body", "mort")),
            P(None, None, ("body", "mort")),
        ),
        out_specs=(P(None, "body", "mort", None), P(None, ("body", "mort"))),
        check_vma=False,
    )
```

```python
import jax
import jax.numpy as jnp
from jax import lax
from jax.experimental import pallas as pl
from jax.experimental.pallas import tpu as pltpu
from jax.sharding import PartitionSpec as P

LANES = 128
ROWS = 8
PIECES = 2
VMEM = pl.BlockSpec(memory_space=pltpu.VMEM)
HBM = pl.BlockSpec(memory_space=pltpu.HBM)


def pieces_of(value):
    out = []
    for _ in range(PIECES - 1):
        part = value.astype(jnp.bfloat16).astype(jnp.float32)
        out.append(part)
        value = value - part
    return out + [value]


def lane_gather(table, index):
    return jnp.take_along_axis(table, index, axis=1, mode="promise_in_bounds")


def split_index(index, size):
    if size & (size - 1):
        return index // size, index % size
    return lax.shift_right_logical(index, size.bit_length() - 1), index & (size - 1)


def onehot(row, count):
    kind = jnp.bfloat16 if count <= 256 else jnp.float32
    ids = lax.broadcasted_iota(jnp.int32, (count, LANES), 0).astype(kind)
    same = row.astype(kind) == ids
    return jnp.where(same, jnp.ones_like(ids), jnp.zeros_like(ids)).astype(jnp.bfloat16)


def start_all(copies):
    for copy in copies:
        copy.start()


def gather_rows(rows, index):
    row, lane = split_index(index, LANES)
    value = None
    for number, piece in enumerate(rows):
        got = lane_gather(jnp.broadcast_to(piece, index.shape), lane)
        value = got if value is None else jnp.where(row == number, got, value)
    return value


def nt_dot(a, b):
    return lax.dot_general(a, b, (((1,), (1,)), ((), ())), preferred_element_type=jnp.float32)


def make_shares(
    disp_ref, gap_ref, weight_ref, basis_ref, cell_ref, seg_ref, owner_ref,
    partial_ref, terms, acc,
):
    count, modes, _ = partial_ref.shape
    _, cells_x, cells_y, _ = disp_ref.shape
    blocks = gap_ref.shape[0]
    segments = partial_ref.shape[2]
    pad = terms.shape[0] // blocks
    per = LANES // cells_y
    lane = lax.broadcasted_iota(jnp.int32, (cells_y, LANES), 1)
    columns = []
    for j in range(per):
        column = jnp.zeros((cells_y, LANES), jnp.float32)
        for r in range(cells_x // per):
            values = disp_ref[2, r * per + j, :, :][:, 0:1]
            column = jnp.where(lane == r, values, column)
        columns.append(column)
    table = jnp.concatenate(columns, axis=0).T
    surface = [table[r : r + 1, :] for r in range(cells_x // per)]

    zero = jnp.zeros((ROWS, LANES), jnp.float32)

    def prepare(t, _):
        first = pl.multiple_of(t * ROWS, ROWS)
        rows = pl.ds(first, ROWS)
        gap = gap_ref[rows, :] + gather_rows(surface, cell_ref[rows, :])
        weights = weight_ref[rows, :]
        for k in range(modes):
            basis = basis_ref[pl.ds(first * modes + k, ROWS, stride=modes), :]
            for s, piece in enumerate(pieces_of(weights * basis * gap)):
                terms[pl.ds(first * pad + s * modes + k, ROWS, stride=pad), :] = piece
        for k in range(PIECES * modes, pad):
            terms[pl.ds(first * pad + k, ROWS, stride=pad), :] = zero
        return 0

    lax.fori_loop(0, blocks // ROWS, prepare, 0, unroll=2)
    acc[...] = jnp.zeros_like(acc)

    def add(t, _):
        first = pl.multiple_of(t * ROWS, ROWS)
        left, right = [], []
        for i in range(ROWS):
            item = terms[pl.ds(pl.multiple_of((first + i) * pad, pad), pad), :]
            owner = owner_ref[first + i]
            left.append(
                jnp.concatenate(
                    [jnp.where(owner == o, item, jnp.zeros_like(item)) for o in range(count)], axis=0
                ).astype(jnp.bfloat16)
            )
            right.append(onehot(seg_ref[pl.ds(first + i, 1), :], segments))
        acc[...] += nt_dot(jnp.concatenate(left, axis=1), jnp.concatenate(right, axis=1))
        return 0

    lax.fori_loop(0, blocks // ROWS, add, 0, unroll=4)
    for o in range(count):
        total = acc[pl.ds(o * pad, pad), :]
        value = total[0:modes]
        for s in range(1, PIECES):
            value = value + total[s * modes : (s + 1) * modes]
        partial_ref[o] = value


def exchange_kernel(
    *refs,
):
    inputs, outputs, held, rest = refs[:12], refs[12:16], refs[16:28], refs[28:]
    (
        disp_ref, cell_ref, gap_ref, weight_ref, basis_ref, owner_ref, seg_ref,
        mult_ref, inv_ref, row_ref, stiff_ref, load_ref,
    ) = held
    changes_ref, updated_ref, base_ref, owners_ref = outputs
    (
        xhalo_ref, yhalo_ref, load_sem, terms, acc, partial_ref, face_ref, landed, send1, recv1, send2, recv2, sendx, recvx, sendy, recvy,
    ) = rest
    loads = [
        pltpu.make_async_copy(source, target, load_sem.at[i])
        for i, (source, target) in enumerate(zip(inputs, held))
    ]
    start_all(loads)
    count, nb = lax.axis_size("mort"), lax.axis_size("body")
    me, mb = lax.axis_index("mort"), lax.axis_index("body")
    cells_x = disp_ref.shape[1]
    barrier = pltpu.get_barrier_semaphore()
    for j in range(1, count):
        pl.semaphore_signal(
            barrier, inc=1, device_id={"mort": lax.rem(me + j, count)},
            device_id_type=pl.DeviceIdType.MESH,
        )
    for j in (1, nb - 1):
        pl.semaphore_signal(
            barrier, inc=1, device_id={"body": lax.rem(mb + j, nb)},
            device_id_type=pl.DeviceIdType.MESH,
        )
    cells_y = disp_ref.shape[2]
    for copy in loads[:-2]:
        copy.wait()
    face_ref[0] = disp_ref[:, :, cells_y - 1, :]
    face_ref[1] = disp_ref[:, :, 0, :]
    make_shares(
        disp_ref, gap_ref, weight_ref, basis_ref, cell_ref, seg_ref, owner_ref,
        partial_ref, terms, acc,
    )
    pl.semaphore_wait(barrier, count + 1)

    def share(j):
        target = lax.rem(me + j, count)
        return pltpu.make_async_remote_copy(
            src_ref=partial_ref.at[target], dst_ref=landed.at[j],
            send_sem=send1.at[j], recv_sem=recv1.at[j],
            device_id={"mort": target}, device_id_type=pl.DeviceIdType.MESH,
        )

    def xcopy(side):
        return pltpu.make_async_remote_copy(
            src_ref=disp_ref.at[:, cells_x - 1 if side == 0 else 0],
            dst_ref=xhalo_ref.at[side],
            send_sem=sendx.at[side], recv_sem=recvx.at[side],
            device_id={"body": lax.rem(mb + (1 if side == 0 else nb - 1), nb)},
            device_id_type=pl.DeviceIdType.MESH,
        )

    def ycopy(side):
        return pltpu.make_async_remote_copy(
            src_ref=face_ref.at[side], dst_ref=yhalo_ref.at[side],
            send_sem=sendy.at[side], recv_sem=recvy.at[side],
            device_id={"mort": lax.rem(me + (1 if side == 0 else count - 1), count)},
            device_id_type=pl.DeviceIdType.MESH,
        )

    shares = [share(j) for j in range(1, count)]
    for copy in shares:
        copy.start()
    halos = []
    for make, place, size, ref in ((xcopy, mb, nb, xhalo_ref), (ycopy, me, count, yhalo_ref)):
        for side in range(2):
            sends = place < size - 1 if side == 0 else place > 0
            takes = place > 0 if side == 0 else place < size - 1
            halos.append((make, side, sends, takes))

            @pl.when(sends)
            def _():
                make(side).start()

            @pl.when(jnp.logical_not(takes))
            def _():
                ref[side] = jnp.zeros(ref.shape[1:], ref.dtype)

    total = partial_ref[me]
    for j in range(1, count):
        shares[j - 1].wait_recv()
        total = total + landed[j]
    applied = inv_ref[:, 0, :] * total[0:1, :]
    for l in range(1, total.shape[0]):
        applied = applied + inv_ref[:, l, :] * total[l : l + 1, :]
    old = mult_ref[...]
    updated = jnp.maximum(old - applied, 0.0)
    updated_ref[...] = updated
    changes_ref[me] = updated - old

    def spread(j):
        return pltpu.make_async_remote_copy(
            src_ref=changes_ref.at[me], dst_ref=changes_ref.at[me],
            send_sem=send2.at[j], recv_sem=recv2.at[j],
            device_id={"mort": lax.rem(me + j, count)}, device_id_type=pl.DeviceIdType.MESH,
        )

    def arrival(j):
        source = lax.rem(me + count - j, count)
        return pltpu.make_async_remote_copy(
            src_ref=changes_ref.at[me], dst_ref=changes_ref.at[source],
            send_sem=send2.at[j], recv_sem=recv2.at[j],
            device_id={"mort": lax.rem(me + j, count)}, device_id_type=pl.DeviceIdType.MESH,
        )

    for j in range(1, count):
        spread(j).start()
    owners_ref[...] = jnp.broadcast_to(row_ref[...], (LANES, row_ref.shape[1])).T
    for copy in loads[-2:]:
        copy.wait()
    for make, side, sends, takes in halos:

        @pl.when(takes)
        def _():
            make(side).wait_recv()

    for i in range(disp_ref.shape[0]):
        for x in range(cells_x):
            base_ref[i, x] = stencil(disp_ref, load_ref, stiff_ref, xhalo_ref, yhalo_ref, i, x)
    for copy in shares:
        copy.wait_send()
    for make, side, sends, takes in halos:

        @pl.when(sends)
        def _():
            make(side).wait_send()

    for j in range(1, count):
        spread(j).wait_send()
        arrival(j).wait_recv()


def stencil(disp_ref, load_ref, stiff_ref, xhalo_ref, yhalo_ref, i, x):
    _, cells_x, cells_y, nz = disp_ref.shape
    lane = lax.broadcasted_iota(jnp.int32, (cells_y, nz), 1)
    row = lax.broadcasted_iota(jnp.int32, (cells_y, nz), 0)
    here = disp_ref[i, x]
    low = disp_ref[i, x - 1] if x > 0 else xhalo_ref[0, i]
    high = disp_ref[i, x + 1] if x < cells_x - 1 else xhalo_ref[1, i]
    below = jnp.where(row == 0, yhalo_ref[0, i, x : x + 1, :], pltpu.roll(here, 1, 0))
    above = jnp.where(
        row == cells_y - 1, yhalo_ref[1, i, x : x + 1, :], pltpu.roll(here, cells_y - 1, 0)
    )
    left = jnp.where(lane == 0, 0.0, pltpu.roll(here, 1, 1))
    right = jnp.where(lane == nz - 1, 0.0, pltpu.roll(here, nz - 1, 1))
    beside = high + low + above + below + right + left
    return load_ref[i, x] - ((6.0 + stiff_ref[x]) * here - beside)


def residual_kernel(
    base_ref, weight_ref, basis_ref, cell_ref, seg_ref, owners, changes_ref, new_ref,
    out_hbm, updated_ref, last_ref, loads, spots, out_sems,
):
    parts, cells_x, cells_y, nz = base_ref.shape
    blocks = weight_ref.shape[0]
    count, modes, segments = changes_ref.shape
    updated_ref[...] = new_ref[...]

    def store(i):
        source = last_ref if i == 2 else base_ref.at[i]
        return pltpu.make_async_copy(source, out_hbm.at[i], out_sems.at[i])

    for i in range(parts):
        if i != 2:
            store(i).start()

    def pressures(t, _):
        first = pl.multiple_of(t * ROWS, ROWS)
        rows = pl.ds(first, ROWS)
        owner = owners[rows, :]
        segs = seg_ref[rows, :]
        masks = [owner == o for o in range(count)]
        pressure = None
        for k in range(modes):
            pieces = []
            for h in range(segments // LANES):
                piece = jnp.zeros((ROWS, LANES), jnp.float32)
                for o in range(count):
                    row = changes_ref[o, k : k + 1, h * LANES : (h + 1) * LANES]
                    piece = jnp.where(masks[o], row, piece)
                pieces.append(piece)
            basis = basis_ref[pl.ds(first * modes + k, ROWS, stride=modes), :]
            term = basis * gather_rows(pieces, segs)
            pressure = term if pressure is None else pressure + term
        for s, piece in enumerate(pieces_of(weight_ref[rows, :] * pressure)):
            loads[s, rows, :] = piece
        for s, spot in enumerate(split_index(cell_ref[rows, :], cells_y)):
            spots[s, rows, :] = spot
        return 0

    lax.fori_loop(0, blocks // ROWS, pressures, 0, unroll=2)
    lane = lax.broadcasted_iota(jnp.int32, (cells_y, nz), 1)
    xs = lax.broadcasted_iota(jnp.int32, (cells_x, LANES), 0)

    def spread(t, acc):
        first = t * ROWS
        left, right = [], []
        for i in range(ROWS):
            place = pl.ds(first + i, 1)
            left.append(onehot(spots[1, place, :], cells_y))
            same = spots[0, place, :] == xs
            right.append(
                jnp.concatenate(
                    [jnp.where(same, loads[s, place, :], 0.0) for s in range(PIECES)], axis=0
                ).astype(jnp.bfloat16)
            )
        return acc + nt_dot(jnp.concatenate(left, axis=1), jnp.concatenate(right, axis=1))

    acc = lax.fori_loop(
        0, blocks // ROWS, spread, jnp.zeros((cells_y, PIECES * cells_x), jnp.float32), unroll=4
    )
    for x in range(cells_x):
        traction = acc[:, x : x + 1]
        for s in range(1, PIECES):
            traction = traction + acc[:, s * cells_x + x : s * cells_x + x + 1]
        residual = base_ref[2, x]
        last_ref[x] = jnp.where(lane == 0, residual + traction, residual)
    store(2).start()
    for i in range(parts):
        store(i).wait()


def body(
    displacement, body_load, stiffness, initial_gap, weights, basis_values, point_cell,
    point_segment, block_owner, multipliers, block_inverse,
):
    parts, cells_x, cells_y, nz = displacement.shape
    blocks, points = initial_gap.shape
    modes, segments = multipliers.shape
    count = lax.axis_size("mort")
    f32 = jnp.float32
    basis = basis_values.reshape(blocks * modes, points)
    pad = -(-PIECES * modes // ROWS) * ROWS
    shape = jax.ShapeDtypeStruct
    dma = pltpu.SemaphoreType.DMA
    sources = (
        displacement, point_cell, initial_gap, weights, basis, block_owner.reshape(blocks),
        point_segment, multipliers, block_inverse, block_owner.reshape(1, blocks), stiffness,
        body_load,
    )
    changes, new, base, owners = pl.pallas_call(
        exchange_kernel,
        name="exchange",
        out_shape=(
            shape((count, modes, segments), f32),
            shape((modes, segments), f32),
            shape(displacement.shape, f32),
            shape((blocks, LANES), jnp.int32),
        ),
        in_specs=[HBM] * len(sources),
        out_specs=(VMEM,) * 4,
        scratch_shapes=[
            pltpu.SMEM(a.shape, a.dtype) if a.ndim == 1 else pltpu.VMEM(a.shape, a.dtype)
            for a in sources
        ]
        + [pltpu.VMEM((2, parts, cells_y, nz), f32), pltpu.VMEM((2, parts, cells_x, nz), f32)]
        + [dma((len(sources),))]
        + [
            pltpu.VMEM((blocks * pad, LANES), f32),
            pltpu.VMEM((count * pad, segments), f32),
            pltpu.VMEM((count, modes, segments), f32),
            pltpu.VMEM((2, parts, cells_x, nz), f32),
            pltpu.VMEM((count, modes, segments), f32),
        ]
        + [dma((count,))] * 4
        + [dma((2,))] * 4,
        compiler_params=pltpu.CompilerParams(
            vmem_limit_bytes=8 << 20, collective_id=0, has_side_effects=True
        ),
    )(*[pltpu.with_memory_space_constraint(a, pltpu.HBM) for a in sources])
    return pl.pallas_call(
        residual_kernel,
        name="residual",
        compiler_params=pltpu.CompilerParams(vmem_limit_bytes=8 << 20),
        out_shape=(
            shape(displacement.shape, f32),
            shape((modes, segments), f32),
        ),
        in_specs=[VMEM] * 8,
        out_specs=(HBM, VMEM),
        scratch_shapes=[
            pltpu.VMEM(displacement.shape[1:], f32),
            pltpu.VMEM((PIECES, blocks, LANES), f32),
            pltpu.VMEM((2, blocks, LANES), jnp.int32),
            dma((parts,)),
        ],
    )(base, weights, basis, point_cell, point_segment, owners, changes, new)


def solution(mesh):
    return jax.shard_map(
        body,
        mesh=mesh,
        in_specs=(
            P(None, "body", "mort", None),
            P(None, "body", "mort", None),
            P("body", "mort", None),
            P(("body", "mort"), None),
            P(("body", "mort"), None),
            P(("body", "mort"), None, None),
            P(("body", "mort"), None),
            P(("body", "mort"), None),
            P(("body", "mort"), None),
            P(None, ("body", "mort")),
            P(None, None, ("body", "mort")),
        ),
        out_specs=(P(None, "body", "mort", None), P(None, ("body", "mort"))),
        check_vma=False,
    )
```

```python
import jax
import jax.numpy as jnp
from jax import lax
from jax.experimental import pallas as pl
from jax.experimental.pallas import tpu as pltpu
from jax.sharding import PartitionSpec as P

LANES = 128
ROWS = 8
PIECES = 2
VMEM = pl.BlockSpec(memory_space=pltpu.VMEM)
HBM = pl.BlockSpec(memory_space=pltpu.HBM)


def pieces_of(value):
    out = []
    for _ in range(PIECES - 1):
        part = value.astype(jnp.bfloat16).astype(jnp.float32)
        out.append(part)
        value = value - part
    return out + [value]


def lane_gather(table, index):
    return jnp.take_along_axis(table, index, axis=1, mode="promise_in_bounds")


def split_index(index, size):
    if size & (size - 1):
        return index // size, index % size
    return lax.shift_right_logical(index, size.bit_length() - 1), index & (size - 1)


def onehot(row, count):
    kind = jnp.bfloat16 if count <= 256 else jnp.float32
    ids = lax.broadcasted_iota(jnp.int32, (count, LANES), 0).astype(kind)
    same = row.astype(kind) == ids
    return jnp.where(same, jnp.ones_like(ids), jnp.zeros_like(ids)).astype(jnp.bfloat16)


def owner_rows(table, owner, gathered):
    count = table.shape[0]
    if count % ROWS or not gathered:
        value = jnp.zeros(owner.shape, table.dtype)
        for o in range(count):
            value = jnp.where(owner == o, table[o : o + 1], value)
        return value
    group, place = split_index(owner, ROWS)
    value = None
    for g in range(count // ROWS):
        rows = table[g * ROWS : (g + 1) * ROWS]
        got = jnp.take_along_axis(rows, place, axis=0, mode="promise_in_bounds")
        value = got if value is None else jnp.where(group == g, got, value)
    return value


def start_all(copies):
    for copy in copies:
        copy.start()


def gather_rows(rows, index):
    row, lane = split_index(index, LANES)
    value = None
    for number, piece in enumerate(rows):
        got = lane_gather(jnp.broadcast_to(piece, index.shape), lane)
        value = got if value is None else jnp.where(row == number, got, value)
    return value


def nt_dot(a, b):
    return lax.dot_general(a, b, (((1,), (1,)), ((), ())), preferred_element_type=jnp.float32)


def make_shares(
    disp_ref, gap_ref, weight_ref, basis_ref, cell_ref, seg_ref, owner_ref,
    partial_ref, terms, acc,
):
    count, modes, _ = partial_ref.shape
    _, cells_x, cells_y, _ = disp_ref.shape
    blocks = gap_ref.shape[0]
    segments = partial_ref.shape[2]
    pad = terms.shape[0] // blocks
    per = LANES // cells_y
    lane = lax.broadcasted_iota(jnp.int32, (cells_y, LANES), 1)
    columns = []
    for j in range(per):
        column = jnp.zeros((cells_y, LANES), jnp.float32)
        for r in range(cells_x // per):
            values = disp_ref[2, r * per + j, :, :][:, 0:1]
            column = jnp.where(lane == r, values, column)
        columns.append(column)
    table = jnp.concatenate(columns, axis=0).T
    surface = [table[r : r + 1, :] for r in range(cells_x // per)]

    zero = jnp.zeros((ROWS, LANES), jnp.float32)

    def prepare(t, _):
        first = pl.multiple_of(t * ROWS, ROWS)
        rows = pl.ds(first, ROWS)
        gap = gap_ref[rows, :] + gather_rows(surface, cell_ref[rows, :])
        weights = weight_ref[rows, :]
        for k in range(modes):
            basis = basis_ref[pl.ds(first * modes + k, ROWS, stride=modes), :]
            for s, piece in enumerate(pieces_of(weights * basis * gap)):
                terms[pl.ds(first * pad + s * modes + k, ROWS, stride=pad), :] = piece
        for k in range(PIECES * modes, pad):
            terms[pl.ds(first * pad + k, ROWS, stride=pad), :] = zero
        return 0

    lax.fori_loop(0, blocks // ROWS, prepare, 0, unroll=2)
    acc[...] = jnp.zeros_like(acc)

    def add(t, _):
        first = pl.multiple_of(t * ROWS, ROWS)
        left, right = [], []
        for i in range(ROWS):
            item = terms[pl.ds(pl.multiple_of((first + i) * pad, pad), pad), :]
            owner = jnp.full((ROWS, LANES), owner_ref[first + i], jnp.int32)
            left.append(
                jnp.concatenate(
                    [jnp.where(owner == o, item, jnp.zeros_like(item)) for o in range(count)], axis=0
                ).astype(jnp.bfloat16)
            )
            right.append(onehot(seg_ref[pl.ds(first + i, 1), :], segments))
        acc[...] += nt_dot(jnp.concatenate(left, axis=1), jnp.concatenate(right, axis=1))
        return 0

    lax.fori_loop(0, blocks // ROWS, add, 0, unroll=4)
    for o in range(count):
        total = acc[pl.ds(o * pad, pad), :]
        value = total[0:modes]
        for s in range(1, PIECES):
            value = value + total[s * modes : (s + 1) * modes]
        partial_ref[o] = value


def exchange_kernel(
    *refs,
):
    inputs, outputs, held, rest = refs[:12], refs[12:16], refs[16:28], refs[28:]
    (
        disp_ref, cell_ref, gap_ref, weight_ref, basis_ref, owner_ref, seg_ref,
        mult_ref, inv_ref, row_ref, stiff_ref, load_ref,
    ) = held
    changes_ref, updated_ref, base_ref, owners_ref = outputs
    (
        xhalo_ref, yhalo_ref, load_sem, terms, acc, partial_ref, face_ref, landed, send1, recv1, send2, recv2, sendx, recvx, sendy, recvy,
    ) = rest
    loads = [
        pltpu.make_async_copy(inputs[i], held[i], load_sem.at[i]) for i in range(1, len(held))
    ]
    surface_load = pltpu.make_async_copy(inputs[0].at[2], disp_ref.at[2], load_sem.at[0])
    side_loads = [
        pltpu.make_async_copy(inputs[0].at[i], disp_ref.at[i], load_sem.at[len(held) + i])
        for i in range(disp_ref.shape[0]) if i != 2
    ]
    surface_load.start()
    start_all(loads[:-2] + side_loads + loads[-2:])
    count, nb = lax.axis_size("mort"), lax.axis_size("body")
    me, mb = lax.axis_index("mort"), lax.axis_index("body")
    cells_x = disp_ref.shape[1]
    barrier = pltpu.get_barrier_semaphore()
    for j in range(1, count):
        pl.semaphore_signal(
            barrier, inc=1, device_id={"mort": lax.rem(me + j, count)},
            device_id_type=pl.DeviceIdType.MESH,
        )
    for j in (1, nb - 1):
        pl.semaphore_signal(
            barrier, inc=1, device_id={"body": lax.rem(mb + j, nb)},
            device_id_type=pl.DeviceIdType.MESH,
        )
    cells_y = disp_ref.shape[2]
    surface_load.wait()
    for copy in loads[:-2]:
        copy.wait()
    make_shares(
        disp_ref, gap_ref, weight_ref, basis_ref, cell_ref, seg_ref, owner_ref,
        partial_ref, terms, acc,
    )
    pl.semaphore_wait(barrier, count + 1)

    def share(j):
        target = lax.rem(me + j, count)
        return pltpu.make_async_remote_copy(
            src_ref=partial_ref.at[target], dst_ref=landed.at[j],
            send_sem=send1.at[j], recv_sem=recv1.at[j],
            device_id={"mort": target}, device_id_type=pl.DeviceIdType.MESH,
        )

    def xcopy(side):
        return pltpu.make_async_remote_copy(
            src_ref=disp_ref.at[:, cells_x - 1 if side == 0 else 0],
            dst_ref=xhalo_ref.at[side],
            send_sem=sendx.at[side], recv_sem=recvx.at[side],
            device_id={"body": lax.rem(mb + (1 if side == 0 else nb - 1), nb)},
            device_id_type=pl.DeviceIdType.MESH,
        )

    def ycopy(side):
        return pltpu.make_async_remote_copy(
            src_ref=face_ref.at[side], dst_ref=yhalo_ref.at[side],
            send_sem=sendy.at[side], recv_sem=recvy.at[side],
            device_id={"mort": lax.rem(me + (1 if side == 0 else count - 1), count)},
            device_id_type=pl.DeviceIdType.MESH,
        )

    shares = [share(j) for j in range(1, count)]
    for copy in shares:
        copy.start()
    for copy in side_loads:
        copy.wait()
    face_ref[0] = disp_ref[:, :, cells_y - 1, :]
    face_ref[1] = disp_ref[:, :, 0, :]
    halos = []
    for make, place, size, ref in ((xcopy, mb, nb, xhalo_ref), (ycopy, me, count, yhalo_ref)):
        for side in range(2):
            sends = place < size - 1 if side == 0 else place > 0
            takes = place > 0 if side == 0 else place < size - 1
            halos.append((make, side, sends, takes))

            @pl.when(sends)
            def _():
                make(side).start()

            @pl.when(jnp.logical_not(takes))
            def _():
                ref[side] = jnp.zeros(ref.shape[1:], ref.dtype)

    total = partial_ref[me]
    for j in range(1, count):
        shares[j - 1].wait_recv()
        total = total + landed[j]
    applied = inv_ref[:, 0, :] * total[0:1, :]
    for l in range(1, total.shape[0]):
        applied = applied + inv_ref[:, l, :] * total[l : l + 1, :]
    old = mult_ref[...]
    updated = jnp.maximum(old - applied, 0.0)
    updated_ref[...] = updated
    changes_ref[me] = updated - old

    def spread(j):
        return pltpu.make_async_remote_copy(
            src_ref=changes_ref.at[me], dst_ref=changes_ref.at[me],
            send_sem=send2.at[j], recv_sem=recv2.at[j],
            device_id={"mort": lax.rem(me + j, count)}, device_id_type=pl.DeviceIdType.MESH,
        )

    def arrival(j):
        source = lax.rem(me + count - j, count)
        return pltpu.make_async_remote_copy(
            src_ref=changes_ref.at[me], dst_ref=changes_ref.at[source],
            send_sem=send2.at[j], recv_sem=recv2.at[j],
            device_id={"mort": lax.rem(me + j, count)}, device_id_type=pl.DeviceIdType.MESH,
        )

    for j in range(1, count):
        spread(j).start()
    owners_ref[...] = jnp.broadcast_to(row_ref[...], (LANES, row_ref.shape[1])).T
    for copy in loads[-2:]:
        copy.wait()
    for make, side, sends, takes in halos:

        @pl.when(takes)
        def _():
            make(side).wait_recv()

    for i in range(disp_ref.shape[0]):
        for x in range(cells_x):
            base_ref[i, x] = stencil(disp_ref, load_ref, stiff_ref, xhalo_ref, yhalo_ref, i, x)
    for copy in shares:
        copy.wait_send()
    for make, side, sends, takes in halos:

        @pl.when(sends)
        def _():
            make(side).wait_send()

    for j in range(1, count):
        spread(j).wait_send()
        arrival(j).wait_recv()


def stencil(disp_ref, load_ref, stiff_ref, xhalo_ref, yhalo_ref, i, x):
    _, cells_x, cells_y, nz = disp_ref.shape
    lane = lax.broadcasted_iota(jnp.int32, (cells_y, nz), 1)
    row = lax.broadcasted_iota(jnp.int32, (cells_y, nz), 0)
    here = disp_ref[i, x]
    low = disp_ref[i, x - 1] if x > 0 else xhalo_ref[0, i]
    high = disp_ref[i, x + 1] if x < cells_x - 1 else xhalo_ref[1, i]
    below = jnp.where(row == 0, yhalo_ref[0, i, x : x + 1, :], pltpu.roll(here, 1, 0))
    above = jnp.where(
        row == cells_y - 1, yhalo_ref[1, i, x : x + 1, :], pltpu.roll(here, cells_y - 1, 0)
    )
    left = jnp.where(lane == 0, 0.0, pltpu.roll(here, 1, 1))
    right = jnp.where(lane == nz - 1, 0.0, pltpu.roll(here, nz - 1, 1))
    beside = high + low + above + below + right + left
    return load_ref[i, x] - ((6.0 + stiff_ref[x]) * here - beside)


def residual_kernel(
    base_ref, weight_ref, basis_ref, cell_ref, seg_ref, owners, changes_ref, new_ref,
    out_hbm, updated_ref, last_ref, loads, spots, out_sems,
):
    parts, cells_x, cells_y, nz = base_ref.shape
    blocks = weight_ref.shape[0]
    count, modes, segments = changes_ref.shape
    updated_ref[...] = new_ref[...]

    def store(i):
        source = last_ref if i == 2 else base_ref.at[i]
        return pltpu.make_async_copy(source, out_hbm.at[i], out_sems.at[i])

    for i in range(parts):
        if i != 2:
            store(i).start()

    tables = [
        [changes_ref[:, k, h * LANES : (h + 1) * LANES] for h in range(segments // LANES)]
        for k in range(modes)
    ]

    def pressures(t, _):
        first = pl.multiple_of(t * ROWS, ROWS)
        rows = pl.ds(first, ROWS)
        owner = owners[rows, :]
        segs = seg_ref[rows, :]
        pressure = None
        for k in range(modes):
            pieces = []
            for h in range(segments // LANES):
                piece = owner_rows(tables[k][h], owner, k < modes // 2)
                pieces.append(piece)
            basis = basis_ref[pl.ds(first * modes + k, ROWS, stride=modes), :]
            term = basis * gather_rows(pieces, segs)
            pressure = term if pressure is None else pressure + term
        for s, piece in enumerate(pieces_of(weight_ref[rows, :] * pressure)):
            loads[s, rows, :] = piece
        for s, spot in enumerate(split_index(cell_ref[rows, :], cells_y)):
            spots[s, rows, :] = spot
        return 0

    lax.fori_loop(0, blocks // ROWS, pressures, 0, unroll=2)
    lane = lax.broadcasted_iota(jnp.int32, (cells_y, nz), 1)
    xs = lax.broadcasted_iota(jnp.int32, (cells_x, LANES), 0)

    def spread(t, acc):
        first = t * ROWS
        left, right = [], []
        for i in range(ROWS):
            place = pl.ds(first + i, 1)
            left.append(onehot(spots[1, place, :], cells_y))
            same = spots[0, place, :] == xs
            right.append(
                jnp.concatenate(
                    [jnp.where(same, loads[s, place, :], 0.0) for s in range(PIECES)], axis=0
                ).astype(jnp.bfloat16)
            )
        return acc + nt_dot(jnp.concatenate(left, axis=1), jnp.concatenate(right, axis=1))

    acc = lax.fori_loop(
        0, blocks // ROWS, spread, jnp.zeros((cells_y, PIECES * cells_x), jnp.float32), unroll=4
    )
    for x in range(cells_x):
        traction = acc[:, x : x + 1]
        for s in range(1, PIECES):
            traction = traction + acc[:, s * cells_x + x : s * cells_x + x + 1]
        residual = base_ref[2, x]
        last_ref[x] = jnp.where(lane == 0, residual + traction, residual)
    store(2).start()
    for i in range(parts):
        store(i).wait()


def body(
    displacement, body_load, stiffness, initial_gap, weights, basis_values, point_cell,
    point_segment, block_owner, multipliers, block_inverse,
):
    parts, cells_x, cells_y, nz = displacement.shape
    blocks, points = initial_gap.shape
    modes, segments = multipliers.shape
    count = lax.axis_size("mort")
    f32 = jnp.float32
    basis = basis_values.reshape(blocks * modes, points)
    pad = -(-PIECES * modes // ROWS) * ROWS
    shape = jax.ShapeDtypeStruct
    dma = pltpu.SemaphoreType.DMA
    sources = (
        displacement, point_cell, initial_gap, weights, basis, block_owner.reshape(blocks),
        point_segment, multipliers, block_inverse, block_owner.reshape(1, blocks), stiffness,
        body_load,
    )
    changes, new, base, owners = pl.pallas_call(
        exchange_kernel,
        name="exchange",
        out_shape=(
            shape((count, modes, segments), f32),
            shape((modes, segments), f32),
            shape(displacement.shape, f32),
            shape((blocks, LANES), jnp.int32),
        ),
        in_specs=[HBM] * len(sources),
        out_specs=(VMEM,) * 4,
        scratch_shapes=[
            pltpu.SMEM(a.shape, a.dtype) if a.ndim == 1 else pltpu.VMEM(a.shape, a.dtype)
            for a in sources
        ]
        + [pltpu.VMEM((2, parts, cells_y, nz), f32), pltpu.VMEM((2, parts, cells_x, nz), f32)]
        + [dma((len(sources) + parts,))]
        + [
            pltpu.VMEM((blocks * pad, LANES), f32),
            pltpu.VMEM((count * pad, segments), f32),
            pltpu.VMEM((count, modes, segments), f32),
            pltpu.VMEM((2, parts, cells_x, nz), f32),
            pltpu.VMEM((count, modes, segments), f32),
        ]
        + [dma((count,))] * 4
        + [dma((2,))] * 4,
        compiler_params=pltpu.CompilerParams(
            vmem_limit_bytes=8 << 20, collective_id=0, has_side_effects=True
        ),
    )(*[pltpu.with_memory_space_constraint(a, pltpu.HBM) for a in sources])
    return pl.pallas_call(
        residual_kernel,
        name="residual",
        compiler_params=pltpu.CompilerParams(vmem_limit_bytes=8 << 20),
        out_shape=(
            shape(displacement.shape, f32),
            shape((modes, segments), f32),
        ),
        in_specs=[VMEM] * 8,
        out_specs=(HBM, VMEM),
        scratch_shapes=[
            pltpu.VMEM(displacement.shape[1:], f32),
            pltpu.VMEM((PIECES, blocks, LANES), f32),
            pltpu.VMEM((2, blocks, LANES), jnp.int32),
            dma((parts,)),
        ],
    )(base, weights, basis, point_cell, point_segment, owners, changes, new)


def solution(mesh):
    return jax.shard_map(
        body,
        mesh=mesh,
        in_specs=(
            P(None, "body", "mort", None),
            P(None, "body", "mort", None),
            P("body", "mort", None),
            P(("body", "mort"), None),
            P(("body", "mort"), None),
            P(("body", "mort"), None, None),
            P(("body", "mort"), None),
            P(("body", "mort"), None),
            P(("body", "mort"), None),
            P(None, ("body", "mort")),
            P(None, None, ("body", "mort")),
        ),
        out_specs=(P(None, "body", "mort", None), P(None, ("body", "mort"))),
        check_vma=False,
    )
```

```python
import jax
import jax.numpy as jnp
from jax import lax
from jax.experimental import pallas as pl
from jax.experimental.pallas import tpu as pltpu
from jax.sharding import PartitionSpec as P

LANES = 128
ROWS = 8
PIECES = 2
VMEM = pl.BlockSpec(memory_space=pltpu.VMEM)
HBM = pl.BlockSpec(memory_space=pltpu.HBM)


def pieces_of(value):
    out = []
    for _ in range(PIECES - 1):
        part = value.astype(jnp.bfloat16).astype(jnp.float32)
        out.append(part)
        value = value - part
    return out + [value]


def lane_gather(table, index):
    return jnp.take_along_axis(table, index, axis=1, mode="promise_in_bounds")


def split_index(index, size):
    if size & (size - 1):
        return index // size, index % size
    return lax.shift_right_logical(index, size.bit_length() - 1), index & (size - 1)


def onehot(row, count):
    kind = jnp.bfloat16 if count <= 256 else jnp.float32
    ids = lax.broadcasted_iota(jnp.int32, (count, LANES), 0).astype(kind)
    same = row.astype(kind) == ids
    return jnp.where(same, jnp.ones_like(ids), jnp.zeros_like(ids)).astype(jnp.bfloat16)


def owner_rows(table, owner, gathered):
    count = table.shape[0]
    if count % ROWS or not gathered:
        value = jnp.zeros(owner.shape, table.dtype)
        for o in range(count):
            value = jnp.where(owner == o, table[o : o + 1], value)
        return value
    group, place = split_index(owner, ROWS)
    value = None
    for g in range(count // ROWS):
        rows = table[g * ROWS : (g + 1) * ROWS]
        got = jnp.take_along_axis(rows, place, axis=0, mode="promise_in_bounds")
        value = got if value is None else jnp.where(group == g, got, value)
    return value


def start_all(copies):
    for copy in copies:
        copy.start()


def gather_rows(rows, index):
    row, lane = split_index(index, LANES)
    value = None
    for number, piece in enumerate(rows):
        got = lane_gather(jnp.broadcast_to(piece, index.shape), lane)
        value = got if value is None else jnp.where(row == number, got, value)
    return value


def nt_dot(a, b):
    return lax.dot_general(a, b, (((1,), (1,)), ((), ())), preferred_element_type=jnp.float32)


def make_shares(
    disp_ref, gap_ref, weight_ref, basis_ref, cell_ref, seg_ref, owner_ref,
    partial_ref, terms, acc,
):
    count, modes, _ = partial_ref.shape
    _, cells_x, cells_y, _ = disp_ref.shape
    blocks = gap_ref.shape[0]
    segments = partial_ref.shape[2]
    pad = terms.shape[0] // blocks
    per = LANES // cells_y
    lane = lax.broadcasted_iota(jnp.int32, (cells_y, LANES), 1)
    columns = []
    for j in range(per):
        column = jnp.zeros((cells_y, LANES), jnp.float32)
        for r in range(cells_x // per):
            values = disp_ref[2, r * per + j, :, :][:, 0:1]
            column = jnp.where(lane == r, values, column)
        columns.append(column)
    table = jnp.concatenate(columns, axis=0).T
    surface = [table[r : r + 1, :] for r in range(cells_x // per)]

    zero = jnp.zeros((ROWS, LANES), jnp.float32)

    def prepare(t, _):
        first = pl.multiple_of(t * ROWS, ROWS)
        rows = pl.ds(first, ROWS)
        gap = gap_ref[rows, :] + gather_rows(surface, cell_ref[rows, :])
        weights = weight_ref[rows, :]
        for k in range(modes):
            basis = basis_ref[pl.ds(first * modes + k, ROWS, stride=modes), :]
            for s, piece in enumerate(pieces_of(weights * basis * gap)):
                terms[pl.ds(first * pad + s * modes + k, ROWS, stride=pad), :] = piece
        for k in range(PIECES * modes, pad):
            terms[pl.ds(first * pad + k, ROWS, stride=pad), :] = zero
        return 0

    lax.fori_loop(0, blocks // ROWS, prepare, 0, unroll=4)
    acc[...] = jnp.zeros_like(acc)

    def add(t, _):
        first = pl.multiple_of(t * ROWS, ROWS)
        left, right = [], []
        for i in range(ROWS):
            item = terms[pl.ds(pl.multiple_of((first + i) * pad, pad), pad), :]
            owner = jnp.full((ROWS, LANES), owner_ref[first + i], jnp.int32)
            high, low = split_index(seg_ref[pl.ds(first + i, 1), :], LANES)
            place = owner * (segments // LANES) + high
            left.append(
                jnp.concatenate(
                    [jnp.where(place == o, item, jnp.zeros_like(item)) for o in range(count * (segments // LANES))], axis=0
                ).astype(jnp.bfloat16)
            )
            right.append(onehot(low, LANES))
        acc[...] += nt_dot(jnp.concatenate(left, axis=1), jnp.concatenate(right, axis=1))
        return 0

    lax.fori_loop(0, blocks // ROWS, add, 0, unroll=8)
    for o in range(count):
        halves = segments // LANES
        total = jnp.concatenate([acc[pl.ds((o * halves + h) * pad, pad), :] for h in range(halves)], axis=1)
        value = total[0:modes]
        for s in range(1, PIECES):
            value = value + total[s * modes : (s + 1) * modes]
        partial_ref[o] = value


def exchange_kernel(
    *refs,
):
    inputs, outputs, held, rest = refs[:12], refs[12:16], refs[16:28], refs[28:]
    (
        disp_ref, cell_ref, gap_ref, weight_ref, basis_ref, owner_ref, seg_ref,
        mult_ref, inv_ref, row_ref, stiff_ref, load_ref,
    ) = held
    changes_ref, updated_ref, base_ref, owners_ref = outputs
    (
        xhalo_ref, yhalo_ref, load_sem, terms, acc, partial_ref, face_ref, landed, send1, recv1, send2, recv2, sendx, recvx, sendy, recvy,
    ) = rest
    loads = [
        pltpu.make_async_copy(inputs[i], held[i], load_sem.at[i]) for i in range(1, len(held))
    ]
    surface_load = pltpu.make_async_copy(inputs[0].at[2], disp_ref.at[2], load_sem.at[0])
    side_loads = [
        pltpu.make_async_copy(inputs[0].at[i], disp_ref.at[i], load_sem.at[len(held) + i])
        for i in range(disp_ref.shape[0]) if i != 2
    ]
    surface_load.start()
    start_all(loads[:-2] + side_loads + loads[-2:])
    count, nb = lax.axis_size("mort"), lax.axis_size("body")
    me, mb = lax.axis_index("mort"), lax.axis_index("body")
    cells_x = disp_ref.shape[1]
    barrier = pltpu.get_barrier_semaphore()
    for j in range(1, count):
        pl.semaphore_signal(
            barrier, inc=1, device_id={"mort": lax.rem(me + j, count)},
            device_id_type=pl.DeviceIdType.MESH,
        )
    for j in (1, nb - 1):
        pl.semaphore_signal(
            barrier, inc=1, device_id={"body": lax.rem(mb + j, nb)},
            device_id_type=pl.DeviceIdType.MESH,
        )
    cells_y = disp_ref.shape[2]
    surface_load.wait()
    for copy in loads[:-2]:
        copy.wait()
    make_shares(
        disp_ref, gap_ref, weight_ref, basis_ref, cell_ref, seg_ref, owner_ref,
        partial_ref, terms, acc,
    )
    pl.semaphore_wait(barrier, count + 1)

    def share(j):
        target = lax.rem(me + j, count)
        return pltpu.make_async_remote_copy(
            src_ref=partial_ref.at[target], dst_ref=landed.at[j],
            send_sem=send1.at[j], recv_sem=recv1.at[j],
            device_id={"mort": target}, device_id_type=pl.DeviceIdType.MESH,
        )

    def xcopy(side):
        return pltpu.make_async_remote_copy(
            src_ref=disp_ref.at[:, cells_x - 1 if side == 0 else 0],
            dst_ref=xhalo_ref.at[side],
            send_sem=sendx.at[side], recv_sem=recvx.at[side],
            device_id={"body": lax.rem(mb + (1 if side == 0 else nb - 1), nb)},
            device_id_type=pl.DeviceIdType.MESH,
        )

    def ycopy(side):
        return pltpu.make_async_remote_copy(
            src_ref=face_ref.at[side], dst_ref=yhalo_ref.at[side],
            send_sem=sendy.at[side], recv_sem=recvy.at[side],
            device_id={"mort": lax.rem(me + (1 if side == 0 else count - 1), count)},
            device_id_type=pl.DeviceIdType.MESH,
        )

    shares = [share(j) for j in range(1, count)]
    for copy in shares:
        copy.start()
    for copy in side_loads:
        copy.wait()
    face_ref[0] = disp_ref[:, :, cells_y - 1, :]
    face_ref[1] = disp_ref[:, :, 0, :]
    halos = []
    for make, place, size, ref in ((xcopy, mb, nb, xhalo_ref), (ycopy, me, count, yhalo_ref)):
        for side in range(2):
            sends = place < size - 1 if side == 0 else place > 0
            takes = place > 0 if side == 0 else place < size - 1
            halos.append((make, side, sends, takes))

            @pl.when(sends)
            def _():
                make(side).start()

            @pl.when(jnp.logical_not(takes))
            def _():
                ref[side] = jnp.zeros(ref.shape[1:], ref.dtype)

    total = partial_ref[me]
    for j in range(1, count):
        shares[j - 1].wait_recv()
        total = total + landed[j]
    applied = inv_ref[:, 0, :] * total[0:1, :]
    for l in range(1, total.shape[0]):
        applied = applied + inv_ref[:, l, :] * total[l : l + 1, :]
    old = mult_ref[...]
    updated = jnp.maximum(old - applied, 0.0)
    updated_ref[...] = updated
    changes_ref[me] = updated - old

    def spread(j):
        return pltpu.make_async_remote_copy(
            src_ref=changes_ref.at[me], dst_ref=changes_ref.at[me],
            send_sem=send2.at[j], recv_sem=recv2.at[j],
            device_id={"mort": lax.rem(me + j, count)}, device_id_type=pl.DeviceIdType.MESH,
        )

    def arrival(j):
        source = lax.rem(me + count - j, count)
        return pltpu.make_async_remote_copy(
            src_ref=changes_ref.at[me], dst_ref=changes_ref.at[source],
            send_sem=send2.at[j], recv_sem=recv2.at[j],
            device_id={"mort": lax.rem(me + j, count)}, device_id_type=pl.DeviceIdType.MESH,
        )

    for j in range(1, count):
        spread(j).start()
    owners_ref[...] = jnp.broadcast_to(row_ref[...], (LANES, row_ref.shape[1])).T
    for copy in loads[-2:]:
        copy.wait()
    for make, side, sends, takes in halos:

        @pl.when(takes)
        def _():
            make(side).wait_recv()

    for i in range(disp_ref.shape[0]):
        for x in range(cells_x):
            base_ref[i, x] = stencil(disp_ref, load_ref, stiff_ref, xhalo_ref, yhalo_ref, i, x)
    for copy in shares:
        copy.wait_send()
    for make, side, sends, takes in halos:

        @pl.when(sends)
        def _():
            make(side).wait_send()

    for j in range(1, count):
        spread(j).wait_send()
        arrival(j).wait_recv()


def stencil(disp_ref, load_ref, stiff_ref, xhalo_ref, yhalo_ref, i, x):
    _, cells_x, cells_y, nz = disp_ref.shape
    lane = lax.broadcasted_iota(jnp.int32, (cells_y, nz), 1)
    row = lax.broadcasted_iota(jnp.int32, (cells_y, nz), 0)
    here = disp_ref[i, x]
    low = disp_ref[i, x - 1] if x > 0 else xhalo_ref[0, i]
    high = disp_ref[i, x + 1] if x < cells_x - 1 else xhalo_ref[1, i]
    below = jnp.where(row == 0, yhalo_ref[0, i, x : x + 1, :], pltpu.roll(here, 1, 0))
    above = jnp.where(
        row == cells_y - 1, yhalo_ref[1, i, x : x + 1, :], pltpu.roll(here, cells_y - 1, 0)
    )
    left = jnp.where(lane == 0, 0.0, pltpu.roll(here, 1, 1))
    right = jnp.where(lane == nz - 1, 0.0, pltpu.roll(here, nz - 1, 1))
    beside = high + low + above + below + right + left
    return load_ref[i, x] - ((6.0 + stiff_ref[x]) * here - beside)


def residual_kernel(
    base_ref, weight_ref, basis_ref, cell_ref, seg_ref, owners, changes_ref, new_ref,
    out_hbm, updated_ref, last_ref, loads, spots, out_sems,
):
    parts, cells_x, cells_y, nz = base_ref.shape
    blocks = weight_ref.shape[0]
    count, modes, segments = changes_ref.shape
    updated_ref[...] = new_ref[...]

    def store(i):
        source = last_ref if i == 2 else base_ref.at[i]
        return pltpu.make_async_copy(source, out_hbm.at[i], out_sems.at[i])

    for i in range(parts):
        if i != 2:
            store(i).start()

    tables = [
        [changes_ref[:, k, h * LANES : (h + 1) * LANES] for h in range(segments // LANES)]
        for k in range(modes)
    ]

    def pressures(t, _):
        first = pl.multiple_of(t * ROWS, ROWS)
        rows = pl.ds(first, ROWS)
        owner = owners[rows, :]
        segs = seg_ref[rows, :]
        pressure = None
        for k in range(modes):
            pieces = []
            for h in range(segments // LANES):
                piece = owner_rows(tables[k][h], owner, k < modes // 2)
                pieces.append(piece)
            basis = basis_ref[pl.ds(first * modes + k, ROWS, stride=modes), :]
            term = basis * gather_rows(pieces, segs)
            pressure = term if pressure is None else pressure + term
        for s, piece in enumerate(pieces_of(weight_ref[rows, :] * pressure)):
            loads[s, rows, :] = piece
        for s, spot in enumerate(split_index(cell_ref[rows, :], cells_y)):
            spots[s, rows, :] = spot
        return 0

    lax.fori_loop(0, blocks // ROWS, pressures, 0, unroll=4)
    lane = lax.broadcasted_iota(jnp.int32, (cells_y, nz), 1)
    xs = lax.broadcasted_iota(jnp.int32, (cells_x, LANES), 0)

    def spread(t, acc):
        first = t * ROWS
        left, right = [], []
        for i in range(ROWS):
            place = pl.ds(first + i, 1)
            left.append(onehot(spots[1, place, :], cells_y))
            same = spots[0, place, :] == xs
            right.append(
                jnp.concatenate(
                    [jnp.where(same, loads[s, place, :], 0.0) for s in range(PIECES)], axis=0
                ).astype(jnp.bfloat16)
            )
        return acc + nt_dot(jnp.concatenate(left, axis=1), jnp.concatenate(right, axis=1))

    acc = lax.fori_loop(
        0, blocks // ROWS, spread, jnp.zeros((cells_y, PIECES * cells_x), jnp.float32), unroll=8
    )
    for x in range(cells_x):
        traction = acc[:, x : x + 1]
        for s in range(1, PIECES):
            traction = traction + acc[:, s * cells_x + x : s * cells_x + x + 1]
        residual = base_ref[2, x]
        last_ref[x] = jnp.where(lane == 0, residual + traction, residual)
    store(2).start()
    for i in range(parts):
        store(i).wait()


def body(
    displacement, body_load, stiffness, initial_gap, weights, basis_values, point_cell,
    point_segment, block_owner, multipliers, block_inverse,
):
    parts, cells_x, cells_y, nz = displacement.shape
    blocks, points = initial_gap.shape
    modes, segments = multipliers.shape
    count = lax.axis_size("mort")
    f32 = jnp.float32
    basis = basis_values.reshape(blocks * modes, points)
    pad = -(-PIECES * modes // ROWS) * ROWS
    shape = jax.ShapeDtypeStruct
    dma = pltpu.SemaphoreType.DMA
    sources = (
        displacement, point_cell, initial_gap, weights, basis, block_owner.reshape(blocks),
        point_segment, multipliers, block_inverse, block_owner.reshape(1, blocks), stiffness,
        body_load,
    )
    changes, new, base, owners = pl.pallas_call(
        exchange_kernel,
        name="exchange",
        out_shape=(
            shape((count, modes, segments), f32),
            shape((modes, segments), f32),
            shape(displacement.shape, f32),
            shape((blocks, LANES), jnp.int32),
        ),
        in_specs=[HBM] * len(sources),
        out_specs=(VMEM,) * 4,
        scratch_shapes=[
            pltpu.SMEM(a.shape, a.dtype) if a.ndim == 1 else pltpu.VMEM(a.shape, a.dtype)
            for a in sources
        ]
        + [pltpu.VMEM((2, parts, cells_y, nz), f32), pltpu.VMEM((2, parts, cells_x, nz), f32)]
        + [dma((len(sources) + parts,))]
        + [
            pltpu.VMEM((blocks * pad, LANES), f32),
            pltpu.VMEM((count * (segments // LANES) * pad, LANES), f32),
            pltpu.VMEM((count, modes, segments), f32),
            pltpu.VMEM((2, parts, cells_x, nz), f32),
            pltpu.VMEM((count, modes, segments), f32),
        ]
        + [dma((count,))] * 4
        + [dma((2,))] * 4,
        compiler_params=pltpu.CompilerParams(
            vmem_limit_bytes=8 << 20, collective_id=0, has_side_effects=True
        ),
    )(*[pltpu.with_memory_space_constraint(a, pltpu.HBM) for a in sources])
    return pl.pallas_call(
        residual_kernel,
        name="residual",
        compiler_params=pltpu.CompilerParams(vmem_limit_bytes=8 << 20),
        out_shape=(
            shape(displacement.shape, f32),
            shape((modes, segments), f32),
        ),
        in_specs=[VMEM] * 8,
        out_specs=(HBM, VMEM),
        scratch_shapes=[
            pltpu.VMEM(displacement.shape[1:], f32),
            pltpu.VMEM((PIECES, blocks, LANES), f32),
            pltpu.VMEM((2, blocks, LANES), jnp.int32),
            dma((parts,)),
        ],
    )(base, weights, basis, point_cell, point_segment, owners, changes, new)


def solution(mesh):
    return jax.shard_map(
        body,
        mesh=mesh,
        in_specs=(
            P(None, "body", "mort", None),
            P(None, "body", "mort", None),
            P("body", "mort", None),
            P(("body", "mort"), None),
            P(("body", "mort"), None),
            P(("body", "mort"), None, None),
            P(("body", "mort"), None),
            P(("body", "mort"), None),
            P(("body", "mort"), None),
            P(None, ("body", "mort")),
            P(None, None, ("body", "mort")),
        ),
        out_specs=(P(None, "body", "mort", None), P(None, ("body", "mort"))),
        check_vma=False,
    )
```
